32 devices in a mesh: au: 8 (over z, core), vert: 4 (over y, x).
Axes of the slice: x: 2, y: 2, z: 4, core: 2. Of those that a mesh axis runs over, the one named last changes fastest.
Arguments:
- vis_value: float32 [128, 128, 2, 128], P('au', 'vert'), may hold values from -6 to 6
- vis_pos: int32 [128, 128, 2, 128], P('au', 'vert'), may hold values from 0 to 1048575, as said below
- counts: int32 [128, 128], P('au', 'vert'), may hold values from 21 to 128, as said below
- kernel: float32 [8, 128], replicated, may hold values from 0.05 to 0.5
Outputs:
- image: float32 [8192, 8192], P(('au', 'vert'))
The draws below stay inside these ranges and needn't reach their ends.
Inputs may be any that keep to these rules, and one draw needn't show every extreme that they name: Slot k of patch (p, q) holds a visibility exactly when k < counts[p, q]; in every draw some patch has all 128 slots live. vis_pos[p, q, 0, k] lies in [p * 64 * 128, (p + 1) * 64 * 128) and vis_pos[p, q, 1, k] in [q * 64 * 128, (q + 1) * 64 * 128), in every slot.
All inputs are finite; a program needn't handle non-finite values.
Results may differ from the reference program's by a relative error of at most 0.0003.
Values sent between devices are 32-bit elements; how exact they have to be, the bound alone decides.
A program may use at most 192 MiB of HBM per device.

```python
import math
import jax
import jax.numpy as jnp
from jax import lax

PATCH = 64
KW = 8
OVER = 128
PR = 128
PCAP = 128
PC = 128


def draw_vis_pos(key, part):
    local_fine = jax.random.randint(key, (PR, PC, 2, PCAP), 0, PATCH * OVER, dtype=jnp.int32)
    row_index = jnp.arange(PR, dtype=jnp.int32)[:, None, None, None]
    col_index = jnp.arange(PC, dtype=jnp.int32)[None, :, None, None]
    component = jnp.arange(2, dtype=jnp.int32)[None, None, :, None]
    patch_base = jnp.where(component == 0, row_index, col_index) * (PATCH * OVER)
    return patch_base + local_fine


def draw_counts(key, part):
    key_counts, key_row, key_col = jax.random.split(jax.random.fold_in(key, 7), 3)
    radius = max(PR // 2, 1)
    row_index = jnp.arange(PR, dtype=jnp.int32)[:, None]
    col_index = jnp.arange(PC, dtype=jnp.int32)[None, :]
    cycle_index = jnp.maximum(jnp.abs(2 * row_index + 1 - PR), jnp.abs(2 * col_index + 1 - PC)) // 2
    scaled = cycle_index * 64 // radius
    ceiling = PCAP * 32 // (32 + scaled)
    drawn_counts = jax.random.randint(key_counts, (PR, PC), ceiling // 2, ceiling + 1, dtype=jnp.int32)
    chosen_row = jax.random.randint(key_row, (), 0, PR, dtype=jnp.int32)
    chosen_col = jax.random.randint(key_col, (), 0, PC, dtype=jnp.int32)
    full_patch = (row_index == chosen_row) & (col_index == chosen_col)
    return jnp.where(full_patch, PCAP, drawn_counts).astype(jnp.int32)


def shard_levels(rng, dims, cuts, least, largest):
    loudness = 1.0
    for position, parts in cuts:
        steps = jax.random.uniform(jax.random.fold_in(jax.random.fold_in(rng, 6), position), (parts,), jnp.float32, least / len(cuts), largest / len(cuts))
        loudness = loudness * jnp.repeat(jnp.exp(steps), dims[position] // parts).reshape((-1,) + (1,) * (len(dims) - 1 - position))
    return loudness


def scatter_about(key, dims, deviation, reach, pieces=(), held_as=jnp.bfloat16):
    result = jax.random.normal(key, dims, jnp.float32) * deviation
    if len(pieces) > 0:
        result = shard_levels(key, dims, pieces, -0.22, 0.18) * result
    return jnp.clip(result, min=-reach, max=reach).astype(held_as)


def setup_inputs(seed: int = 0) -> dict:
    key_of = jax.random.split(jax.random.key(seed), 5)
    vis_value = scatter_about(key_of[0], (PR, PC, 2, PCAP), 1.0, 6.0, ((0, 8), (1, 4)), jnp.float32)
    vis_pos = draw_vis_pos(jax.random.fold_in(key_of[4], 71), 0)
    counts = draw_counts(jax.random.fold_in(key_of[4], 71), 0)
    kernel = jnp.clip(jax.random.uniform(key_of[3], (KW, OVER), jnp.float32, 0.05, 0.5), 0.05, 0.5)
    return {"vis_value": vis_value, "vis_pos": vis_pos, "counts": counts, "kernel": kernel}


def reference(vis_value, vis_pos, counts, kernel):
    kernel_width, oversample = kernel.shape
    grid_size = PR * PATCH
    extent = PATCH + kernel_width
    slot_count = vis_value.shape[3]
    tap_table = kernel.T

    def one_row(pending, row_number):
        values = lax.dynamic_index_in_dim(vis_value, row_number, 0, keepdims=False)
        positions = lax.dynamic_index_in_dim(vis_pos, row_number, 0, keepdims=False)
        tallies = lax.dynamic_index_in_dim(counts, row_number, 0, keepdims=False)
        cell_index = positions // oversample
        fine_index = positions - cell_index * oversample
        offsets = cell_index % PATCH
        tap_values = tap_table[fine_index]
        live_mask = (jnp.arange(slot_count, dtype=jnp.int32)[None, :] < tallies[:, None]).astype(jnp.float32)
        distance = jnp.arange(extent, dtype=jnp.int32)[None, None, None, :] - offsets[..., None]
        weights = jnp.zeros(distance.shape, jnp.float32)
        for tap_step in range(kernel_width):
            weights = weights + jnp.where(distance == tap_step, tap_values[..., tap_step:tap_step + 1], 0.0)
        row_weights = weights[:, 0] * live_mask[:, :, None]
        scaled = values[:, :, :, None] * weights[:, 1][:, None]
        patches = jnp.einsum('nki,nckj->ncij', row_weights, scaled, precision=lax.Precision.HIGHEST)
        core_part = patches[..., :PATCH].transpose(1, 2, 0, 3)
        spill_cols = jnp.pad(patches[..., PATCH:].transpose(1, 2, 0, 3), ((0, 0), (0, 0), (0, 0), (0, PATCH - kernel_width)))
        band_field = jnp.pad(core_part, ((0, 0), (0, 0), (0, 1), (0, 0))) + jnp.pad(spill_cols, ((0, 0), (0, 0), (1, 0), (0, 0)))
        band_field = band_field.reshape(2, extent, (PC + 1) * PATCH)[:, :, :grid_size]
        band_field = band_field.at[:, :kernel_width].add(pending)
        finished = band_field[:, :PATCH]
        complex_rows = finished[0] + 1j * finished[1]
        spectrum = jnp.fft.ifft(complex_rows, axis=1) * grid_size
        return (band_field[:, PATCH:], spectrum)
    start_rim = jnp.zeros((2, kernel_width, grid_size), jnp.float32)
    _, spectra = lax.scan(one_row, start_rim, jnp.arange(PR, dtype=jnp.int32))
    spectra = spectra.reshape(grid_size, grid_size)
    block_size = min(512, grid_size)
    image_scale = 1.0 / math.sqrt(PR * PC * slot_count)

    def one_block(offset_start):
        column_block = lax.dynamic_slice_in_dim(spectra, offset_start, block_size, 1)
        return ((jnp.fft.ifft(column_block, axis=0) * grid_size).real.T * image_scale).astype(jnp.float32)
    images = lax.map(one_block, jnp.arange(grid_size // block_size, dtype=jnp.int32) * block_size)
    return images.reshape(grid_size, grid_size)
```

```python
import math

import jax
import jax.numpy as jnp
from jax import lax
from jax.sharding import PartitionSpec as P

PATCH = 64
PR = 128
PC = 128


highest = lax.Precision.HIGH


def passed_along(value, axis, steps):
    count = lax.axis_size(axis)
    initial, last = (max(0, -steps), min(count, count - steps))
    return lax.ppermute(value, axis, [(source, source + steps) for source in range(initial, last)])


def fourier(length):
    index_list = jnp.arange(length, dtype=jnp.int32)
    angles = (
        2.0
        * math.pi
        / length
        * (index_list[:, None] * index_list[None, :] % length).astype(jnp.float32)
    )
    return jnp.stack([jnp.cos(angles), jnp.sin(angles)])


def twiddle(outer_size, inner_size, length):
    row_index = jnp.arange(outer_size, dtype=jnp.int32)[:, None]
    col_index = jnp.arange(inner_size, dtype=jnp.int32)[None, :]
    angles = 2.0 * math.pi / length * (row_index * col_index % length).astype(jnp.float32)
    return (jnp.cos(angles), jnp.sin(angles))


def complex_table(length):
    cos, sin = fourier(length)
    return jnp.stack([jnp.stack([cos, -sin]), jnp.stack([sin, cos])])


def row_transform(field):
    band_count, outer_size, _, rows, inner_size = field.shape
    length = outer_size * inner_size
    turn_cos, turn_sin = twiddle(outer_size, inner_size, length)
    product = jnp.einsum(
        "scaq,bqcip->sbiap", complex_table(outer_size), field, precision=highest
    )
    rotated = jnp.stack(
        [
            product[0] * turn_cos - product[1] * turn_sin,
            product[0] * turn_sin + product[1] * turn_cos,
        ]
    )
    result = jnp.einsum(
        "scyp,cbiap->sbiya", complex_table(inner_size), rotated, precision=highest
    )
    return result.reshape(2, band_count * rows, length)


def column_transform(received, image_scale):
    length = received.shape[1]
    item_count = received.shape[3]
    inner_size = 128
    outer_size = length // inner_size
    turn_cos, turn_sin = twiddle(outer_size, inner_size, length)
    blocked = received.reshape(2, outer_size, inner_size, item_count)
    product = jnp.einsum(
        "scaq,cqpy->sapy", complex_table(outer_size), blocked, precision=highest
    )
    turn_cos = turn_cos[..., None]
    turn_sin = turn_sin[..., None]
    rotated = jnp.stack(
        [
            product[0] * turn_cos - product[1] * turn_sin,
            product[0] * turn_sin + product[1] * turn_cos,
        ]
    )
    last_table = complex_table(inner_size)[0] * image_scale
    image_rows = jnp.einsum("cbp,capy->yba", last_table, rotated, precision=highest)
    return image_rows.reshape(item_count, length)


def joined(array, group):
    count, lead, slots = array.shape
    blocks = array.reshape(count // group, group, lead, slots)
    before = jnp.roll(blocks[:, group - 1], 1, axis=0)
    return jnp.concatenate([before] + [blocks[:, step] for step in range(group)], axis=-1)


def spread(distance, taps):
    weights = jnp.zeros(distance.shape, jnp.float32)
    for tap_step in range(taps.shape[1]):
        weights = jnp.where(distance == tap_step, taps[:, tap_step][:, None], weights)
    return weights


def band_tiles(values, positions, counts, kernel):
    kernel_width, oversample = kernel.shape
    column_count, _, slot_count = values.shape
    width = 128
    group = width // PATCH
    group_count = column_count // group
    live_mask = jnp.arange(slot_count, dtype=jnp.int32)[None, :] < counts[:, None]
    cell_index = positions // oversample
    fine_index = positions - cell_index * oversample
    selector = (
        fine_index[:, :, None, :] == jnp.arange(oversample, dtype=jnp.int32)[:, None]
    ).astype(jnp.float32)
    taps = jnp.einsum("to,naok->natk", kernel, selector, precision=highest)
    taps = joined(taps.reshape(column_count, 2 * kernel_width, slot_count), group)
    cells = joined(cell_index, group)
    scaled = joined(jnp.where(live_mask[:, None], values, 0.0), group)
    extent = PATCH + kernel_width
    row_distance = (
        jnp.arange(extent, dtype=jnp.int32)[None, :, None] - (cells[:, 0] % PATCH)[:, None]
    )
    starts = jnp.arange(group_count, dtype=jnp.int32) * width
    columns = starts[:, None] + jnp.arange(width, dtype=jnp.int32)
    column_distance = columns[:, :, None] - cells[:, 1][:, None]
    row_weights = spread(row_distance, taps[:, :kernel_width])
    column_weights = spread(column_distance, taps[:, kernel_width:])
    scaled_rows = scaled[:, :, None] * row_weights[:, None]
    return jnp.einsum("mcik,mjk->mcij", scaled_rows, column_weights, precision=highest)


def local(vis_value, vis_pos, counts, kernel):
    kernel_width = kernel.shape[0]
    device_count = lax.axis_size("au") * lax.axis_size("vert")
    slot_count = vis_value.shape[3]
    image_scale = 1.0 / math.sqrt(PR * PC * slot_count)
    vert_count = lax.axis_size("vert")
    band_count = vis_value.shape[0] // vert_count
    local_columns = vis_value.shape[1]
    moved_values = lax.all_to_all(
        vis_value.reshape(vert_count, band_count, local_columns, 2, slot_count),
        "vert",
        split_axis=0,
        concat_axis=2,
        tiled=True,
    )
    positions, tallies = (
        lax.all_to_all(
            vis_pos.reshape(vert_count, band_count, local_columns, 2, slot_count),
            "vert",
            split_axis=0,
            concat_axis=2,
            tiled=True,
        ),
        lax.all_to_all(
            counts.reshape(vert_count, band_count, local_columns),
            "vert",
            split_axis=0,
            concat_axis=2,
            tiled=True,
        ),
    )
    column_count = local_columns * vert_count
    values = moved_values.reshape(band_count, column_count, 2, slot_count)
    positions = positions.reshape(band_count, column_count, 2, slot_count)
    tallies = tallies.reshape(band_count, column_count)
    tiles = lax.map(lambda members: band_tiles(*members, kernel), (values, positions, tallies))
    spill = tiles[..., PATCH:, :]
    arrived = passed_along(spill[-1], ("au", "vert"), 1)
    above = jnp.concatenate([arrived[None], spill[:-1]], axis=0)
    field = jnp.concatenate(
        [tiles[..., :kernel_width, :] + above, tiles[..., kernel_width:PATCH, :]], axis=3
    )
    row_field = row_transform(field)
    length = row_field.shape[2]
    column_share = length // device_count
    return column_transform(
        lax.all_to_all(
            row_field.reshape(2, row_field.shape[1], device_count, column_share),
            ("au", "vert"),
            split_axis=2,
            concat_axis=1,
            tiled=True,
        ),
        image_scale,
    )


def solution(mesh):
    in_specs = (P("au", "vert", None, None), P("au", "vert", None, None), P("au", "vert"), P())
    out_specs = P(("au", "vert"), None)
    return jax.shard_map(local, mesh=mesh, in_specs=in_specs, out_specs=out_specs, check_vma=False)
```

```python
import math

import jax
import jax.numpy as jnp
from jax import lax
from jax.sharding import PartitionSpec as P

PATCH = 64
PR = 128
PC = 128


highest = lax.Precision.HIGH


def passed_along(value, axis, steps):
    count = lax.axis_size(axis)
    initial, last = (max(0, -steps), min(count, count - steps))
    return lax.ppermute(value, axis, [(source, source + steps) for source in range(initial, last)])


def fourier(length):
    index_list = jnp.arange(length, dtype=jnp.int32)
    angles = (
        2.0
        * math.pi
        / length
        * (index_list[:, None] * index_list[None, :] % length).astype(jnp.float32)
    )
    return jnp.stack([jnp.cos(angles), jnp.sin(angles)])


def twiddle(outer_size, inner_size, length):
    row_index = jnp.arange(outer_size, dtype=jnp.int32)[:, None]
    col_index = jnp.arange(inner_size, dtype=jnp.int32)[None, :]
    angles = 2.0 * math.pi / length * (row_index * col_index % length).astype(jnp.float32)
    return (jnp.cos(angles), jnp.sin(angles))


def complex_table(length):
    cos, sin = fourier(length)
    return jnp.stack([jnp.stack([cos, -sin]), jnp.stack([sin, cos])])


def row_transform(field):
    band_count, outer_size, _, rows, inner_size = field.shape
    length = outer_size * inner_size
    turn_cos, turn_sin = twiddle(outer_size, inner_size, length)
    product = jnp.einsum(
        "scaq,bqcip->sbiap", complex_table(outer_size), field, precision=highest
    )
    rotated = jnp.stack(
        [
            product[0] * turn_cos - product[1] * turn_sin,
            product[0] * turn_sin + product[1] * turn_cos,
        ]
    )
    result = jnp.einsum(
        "scyp,cbiap->sbiya", complex_table(inner_size), rotated, precision=highest
    )
    return result.reshape(2, band_count * rows, length)


def column_transform(received, image_scale):
    length = received.shape[1]
    item_count = received.shape[3]
    inner_size = length // 128
    outer_size = length // inner_size
    turn_cos, turn_sin = twiddle(outer_size, inner_size, length)
    blocked = received.reshape(2, outer_size, inner_size, item_count)
    product = jnp.einsum(
        "scaq,cqpy->sapy", complex_table(outer_size), blocked, precision=highest
    )
    turn_cos = turn_cos[..., None]
    turn_sin = turn_sin[..., None]
    rotated = jnp.stack(
        [
            product[0] * turn_cos - product[1] * turn_sin,
            product[0] * turn_sin + product[1] * turn_cos,
        ]
    )
    last_table = complex_table(inner_size)[0] * image_scale
    image_rows = jnp.einsum("cbp,capy->yba", last_table, rotated, precision=highest)
    return image_rows.reshape(item_count, length)


def joined(array, group):
    count, lead, slots = array.shape
    blocks = array.reshape(count // group, group, lead, slots)
    before = jnp.roll(blocks[:, group - 1], 1, axis=0)
    return jnp.concatenate([before] + [blocks[:, step] for step in range(group)], axis=-1)


def spread(distance, taps):
    weights = jnp.zeros(distance.shape, jnp.float32)
    for tap_step in range(taps.shape[1]):
        weights = jnp.where(distance == tap_step, taps[:, tap_step][:, None], weights)
    return weights


def band_tiles(values, positions, counts, kernel):
    kernel_width, oversample = kernel.shape
    column_count, _, slot_count = values.shape
    width = 128
    group = width // PATCH
    group_count = column_count // group
    live_mask = jnp.arange(slot_count, dtype=jnp.int32)[None, :] < counts[:, None]
    cell_index = positions // oversample
    fine_index = positions - cell_index * oversample
    selector = (
        fine_index[:, :, None, :] == jnp.arange(oversample, dtype=jnp.int32)[:, None]
    ).astype(jnp.float32)
    taps = jnp.einsum("to,naok->natk", kernel, selector, precision=highest)
    taps = joined(taps.reshape(column_count, 2 * kernel_width, slot_count), group)
    cells = joined(cell_index, group)
    scaled = joined(jnp.where(live_mask[:, None], values, 0.0), group)
    extent = PATCH + kernel_width
    row_distance = (
        jnp.arange(extent, dtype=jnp.int32)[None, :, None] - (cells[:, 0] % PATCH)[:, None]
    )
    starts = jnp.arange(group_count, dtype=jnp.int32) * width
    columns = starts[:, None] + jnp.arange(width, dtype=jnp.int32)
    column_distance = columns[:, :, None] - cells[:, 1][:, None]
    row_weights = spread(row_distance, taps[:, :kernel_width])
    column_weights = spread(column_distance, taps[:, kernel_width:])
    scaled_rows = scaled[:, :, None] * row_weights[:, None]
    return jnp.einsum("mcik,mjk->mcij", scaled_rows, column_weights, precision=highest)


def local(vis_value, vis_pos, counts, kernel):
    kernel_width = kernel.shape[0]
    device_count = lax.axis_size("au") * lax.axis_size("vert")
    slot_count = vis_value.shape[3]
    image_scale = 1.0 / math.sqrt(PR * PC * slot_count)
    vert_count = lax.axis_size("vert")
    band_count = vis_value.shape[0] // vert_count
    local_columns = vis_value.shape[1]
    moved_values = lax.all_to_all(
        vis_value.reshape(vert_count, band_count, local_columns, 2, slot_count),
        "vert",
        split_axis=0,
        concat_axis=2,
        tiled=True,
    )
    positions, tallies = (
        lax.all_to_all(
            vis_pos.reshape(vert_count, band_count, local_columns, 2, slot_count),
            "vert",
            split_axis=0,
            concat_axis=2,
            tiled=True,
        ),
        lax.all_to_all(
            counts.reshape(vert_count, band_count, local_columns),
            "vert",
            split_axis=0,
            concat_axis=2,
            tiled=True,
        ),
    )
    column_count = local_columns * vert_count
    values = moved_values.reshape(band_count, column_count, 2, slot_count)
    positions = positions.reshape(band_count, column_count, 2, slot_count)
    tallies = tallies.reshape(band_count, column_count)
    tiles = lax.map(lambda members: band_tiles(*members, kernel), (values, positions, tallies))
    spill = tiles[..., PATCH:, :]
    arrived = passed_along(spill[-1], ("au", "vert"), 1)
    above = jnp.concatenate([arrived[None], spill[:-1]], axis=0)
    field = jnp.concatenate(
        [tiles[..., :kernel_width, :] + above, tiles[..., kernel_width:PATCH, :]], axis=3
    )
    row_field = row_transform(field)
    length = row_field.shape[2]
    column_share = length // device_count
    return column_transform(
        lax.all_to_all(
            row_field.reshape(2, row_field.shape[1], device_count, column_share),
            ("au", "vert"),
            split_axis=2,
            concat_axis=1,
            tiled=True,
        ),
        image_scale,
    )


def solution(mesh):
    in_specs = (P("au", "vert", None, None), P("au", "vert", None, None), P("au", "vert"), P())
    out_specs = P(("au", "vert"), None)
    return jax.shard_map(local, mesh=mesh, in_specs=in_specs, out_specs=out_specs, check_vma=False)
```
